32 devices in a mesh: replica: 4 (over z), row: 4 (over y, x), col: 2 (over core).
Axes of the slice: x: 2, y: 2, z: 4, core: 2. Of those that a mesh axis runs over, the one named last changes fastest.
Arguments:
- hidden: bfloat16 [4, 1408, 14336], P('replica', 'col', 'row'), may hold values from -6 to 6
- cotangent: bfloat16 [4, 1408, 4096], P('replica', 'row', 'col'), may hold values from -6 to 6
- weight: bfloat16 [4, 14336, 4096], P('replica', 'row', 'col'), may hold values from -6 to 6
- prev_weight: bfloat16 [4, 14336, 4096], P('replica', 'row', 'col'), may hold values from -6 to 6
- prev_grad: bfloat16 [4, 14336, 4096], P('replica', 'row', 'col'), may hold values from -3 to 3
Outputs:
- output: bfloat16 [4, 1408, 4096], P('replica', 'row', 'col')
- hidden_grad: bfloat16 [4, 1408, 14336], P('replica', 'col', 'row')
- new_weight: bfloat16 [4, 14336, 4096], P('replica', 'row', 'col')
The draws below stay inside these ranges and needn't reach their ends.
All inputs are finite; a program needn't handle non-finite values.
Results may differ from the reference program's by a relative error of at most 0.017.
Values may be sent and summed in bfloat16 or wider, within the bound.
A program may use at most 192 MiB of HBM per device.

```python
import jax
import jax.numpy as jnp
from jax import lax

D = 4096
FF = 14336
TOK_GROUP = 1408
N_REPLICA = 4
N_ROW = 4
N_COL = 2


def level_of(stream_key, shape, pieces, smallest, high):
    level, own = 1.0, jax.random.fold_in(stream_key, 6)
    for position, shards_of in pieces:
        draws = jnp.exp(jax.random.uniform(jax.random.fold_in(own, position), (shards_of,), jnp.float32, smallest / len(pieces), high / len(pieces)))
        level = level * jnp.repeat(draws, shape[position] // shards_of).reshape([-1 if axis == position else 1 for axis in range(len(shape))])
    return level


def gaussian(stream_key, dims, width, limit, pieces=(), kind=jnp.bfloat16):
    drawn = jax.random.normal(stream_key, dims, jnp.float32) * width
    if len(pieces) > 0:
        drawn = level_of(stream_key, dims, pieces, -0.22, 0.18) * drawn
    return jnp.clip(drawn, min=-limit, max=limit).astype(kind)


def setup_inputs(seed: int = 0) -> dict:
    key_of = jax.random.split(jax.random.key(seed), 6)
    return {
        "hidden": gaussian(key_of[0], (N_REPLICA, TOK_GROUP, FF), 1.0, 6.0, ((0, 4), (1, 2), (2, 4))),
        "cotangent": gaussian(key_of[1], (N_REPLICA, TOK_GROUP, D), 1.0, 6.0, ((0, 4), (1, 4), (2, 2))),
        "weight": gaussian(key_of[2], (N_REPLICA, FF, D), 1.0, 6.0, ((0, 4), (1, 4), (2, 2))),
        "prev_weight": gaussian(key_of[3], (N_REPLICA, FF, D), 1.0, 6.0, ((0, 4), (1, 4), (2, 2))),
        "prev_grad": gaussian(key_of[4], (N_REPLICA, FF, D), 0.5, 3.0, ((0, 4), (1, 4), (2, 2))),
    }


def reference(hidden, cotangent, weight, prev_weight, prev_grad):
    scale = FF ** -0.5
    row_width = FF // N_ROW
    col_width = D // N_COL

    def blended(index):
        value = weight[index].astype(jnp.float32) - 0.5 * prev_weight[index].astype(jnp.float32)
        return value.astype(jnp.bfloat16).astype(jnp.float32)

    def one_replica(index):
        inputs = hidden[index]
        upstream = cotangent[index]
        matrix = weight[index]

        def forward_block(block, total):
            start = (block * row_width).astype(jnp.int32)
            piece_in = lax.dynamic_slice_in_dim(inputs, start, row_width, 1)
            piece_w = lax.dynamic_slice_in_dim(matrix, start, row_width, 0)
            term = jnp.dot(piece_in, piece_w, preferred_element_type=jnp.float32) * scale
            return total + term.astype(jnp.bfloat16).astype(jnp.float32)

        output = lax.fori_loop(0, N_ROW, forward_block, jnp.zeros((TOK_GROUP, D), jnp.float32)).astype(jnp.bfloat16)

        def backward_block(block, total):
            start = (block * col_width).astype(jnp.int32)
            piece_up = lax.dynamic_slice_in_dim(upstream, start, col_width, 1)
            piece_w = lax.dynamic_slice_in_dim(matrix, start, col_width, 1)
            term = lax.dot_general(piece_up, piece_w, (((1,), (1,)), ((), ())), preferred_element_type=jnp.float32) * scale
            return total + term.astype(jnp.bfloat16).astype(jnp.float32)

        hidden_grad = lax.fori_loop(0, N_COL, backward_block, jnp.zeros((TOK_GROUP, FF), jnp.float32)).astype(jnp.bfloat16)
        grad = lax.dot_general(inputs, upstream, (((0,), (0,)), ((), ())), preferred_element_type=jnp.float32) * scale
        count = jnp.int32(N_REPLICA)
        left = blended(((index - 1) % count).astype(jnp.int32))
        right = blended(((index + 1) % count).astype(jnp.int32))
        centre = blended(index)
        fresh = centre + (left + centre + right) / 3.0 - 0.5 * (grad - prev_grad[index].astype(jnp.float32))
        return output, hidden_grad, fresh.astype(jnp.bfloat16)

    output, hidden_grad, new_weight = lax.map(one_replica, jnp.arange(N_REPLICA, dtype=jnp.int32))
    return (output, hidden_grad, new_weight)
```

```python
import jax
import jax.numpy as jnp
from jax import lax
from jax.sharding import PartitionSpec as P


FF = 14336
PARTS = (2, 22, 26, 5, 1)
DIRECT = 4


def shifted(array, axis, by):
    peers = lax.axis_size(axis)
    return lax.ppermute(array, axis, [(i, (i + by) % peers) for i in range(peers)])


def gather_rows(block, axis):
    peers = lax.axis_size(axis)
    if peers > DIRECT:
        return lax.all_gather(block, axis, axis=0, tiled=True)
    me, size = lax.axis_index(axis), block.shape[0]
    whole = jnp.zeros((peers * size, block.shape[1]), block.dtype)
    whole = lax.dynamic_update_slice(whole, block, (me * size, 0))
    for step in range(1, peers):
        other = shifted(block, axis, step)
        owner = lax.rem(me - step + peers, peers)
        whole = lax.dynamic_update_slice(whole, other, (owner * size, 0))
    return whole


def sum_rows(partial, axis):
    peers = lax.axis_size(axis)
    if peers > DIRECT:
        return lax.psum_scatter(partial, axis, scatter_dimension=0, tiled=True)
    me, size = lax.axis_index(axis), partial.shape[0] // peers

    def block(owner):
        return lax.dynamic_slice_in_dim(partial, owner * size, size, 0)

    total = block(me).astype(jnp.float32)
    for step in range(1, peers):
        total += shifted(block(lax.rem(me + step, peers)), axis, step).astype(jnp.float32)
    return total.astype(partial.dtype)


def row_chunks(rows):
    total = sum(PARTS)
    if rows % (16 * total):
        return [(0, rows)]
    unit, at, chunks = rows // total, 0, []
    for part in PARTS:
        chunks.append((at, part * unit))
        at += part * unit
    return chunks


def on_device(hidden, cotangent, weight, prev_weight, prev_grad):
    scale = FF ** (-0.5)
    matrix, before, slope = weight[0], prev_weight[0], prev_grad[0]
    rows = matrix.shape[0]
    chunks = row_chunks(rows)

    lefts, rights = [], []
    for at, size in chunks:
        piece = (
            matrix[at : at + size].astype(jnp.float32)
            - 0.5 * before[at : at + size].astype(jnp.float32)
        ).astype(jnp.bfloat16)
        lefts.append(shifted(piece, "replica", 1))
        rights.append(shifted(piece, "replica", -1))

    gathered = gather_rows(hidden[0], "col")
    upstream = gather_rows(cotangent[0], "row")
    partial_value = (
        jnp.dot(gathered, matrix, preferred_element_type=jnp.float32) * scale
    ).astype(jnp.bfloat16)
    output = sum_rows(partial_value, "row")
    term = (
        lax.dot_general(
            upstream, matrix, (((1,), (1,)), ((), ())), preferred_element_type=jnp.float32
        )
        * scale
    )
    hidden_grad = sum_rows(term.astype(jnp.bfloat16), "col")
    grad = (
        lax.dot_general(
            gathered, upstream, (((0,), (0,)), ((), ())), preferred_element_type=jnp.float32
        )
        * scale
    )
    own = (
        matrix.astype(jnp.float32) - 0.5 * before.astype(jnp.float32)
    ).astype(jnp.bfloat16).astype(jnp.float32)
    base = own * (4.0 / 3.0) - 0.5 * (grad - slope.astype(jnp.float32))
    base, output, hidden_grad = lax.optimization_barrier((base, output, hidden_grad))

    fresh = jnp.zeros(matrix.shape, jnp.bfloat16)
    for (at, size), left, right in zip(chunks, lefts, rights):
        around = (left.astype(jnp.float32) + right.astype(jnp.float32)) * (1.0 / 3.0)
        piece = (base[at : at + size] + around).astype(jnp.bfloat16)
        fresh = lax.dynamic_update_slice(fresh, piece, (at, 0))
    return (output[None], hidden_grad[None], fresh[None])


def solution(mesh):
    placed = (
        P("replica", "col", "row"),
        P("replica", "row", "col"),
        P("replica", "row", "col"),
        P("replica", "row", "col"),
        P("replica", "row", "col"),
    )
    return jax.shard_map(
        on_device,
        mesh=mesh,
        in_specs=placed,
        out_specs=(
            P("replica", "row", "col"),
            P("replica", "col", "row"),
            P("replica", "row", "col"),
        ),
        check_vma=False,
    )
```

```python
import jax
import jax.numpy as jnp
from jax import lax
from jax.sharding import PartitionSpec as P


FF = 14336
PARTS = (1, 7, 20, 23, 4.5, 0.5)
DIRECT = 4


def shifted(array, axis, by):
    peers = lax.axis_size(axis)
    return lax.ppermute(array, axis, [(i, (i + by) % peers) for i in range(peers)])


def gather_rows(block, axis):
    peers = lax.axis_size(axis)
    if peers > DIRECT:
        return lax.all_gather(block, axis, axis=0, tiled=True)
    me, size = lax.axis_index(axis), block.shape[0]
    whole = jnp.zeros((peers * size, block.shape[1]), block.dtype)
    whole = lax.dynamic_update_slice(whole, block, (me * size, 0))
    for step in range(1, peers):
        other = shifted(block, axis, step)
        owner = lax.rem(me - step + peers, peers)
        whole = lax.dynamic_update_slice(whole, other, (owner * size, 0))
    return whole


def sum_rows(partial, axis):
    peers = lax.axis_size(axis)
    if peers > DIRECT:
        return lax.psum_scatter(partial, axis, scatter_dimension=0, tiled=True)
    me, size = lax.axis_index(axis), partial.shape[0] // peers

    def block(owner):
        return lax.dynamic_slice_in_dim(partial, owner * size, size, 0)

    total = block(me).astype(jnp.float32)
    for step in range(1, peers):
        total += shifted(block(lax.rem(me + step, peers)), axis, step).astype(jnp.float32)
    return total.astype(partial.dtype)


def row_chunks(rows):
    total = int(sum(PARTS))
    if rows % (16 * total):
        return [(0, rows)]
    unit, at, chunks = int(rows // total), 0, []
    for part in PARTS[:-2]:
        chunks.append((at, part * unit))
        at += part * unit
    last = max(16, unit // 2)
    chunks.append((at, rows - last - at))
    chunks.append((rows - last, last))
    return chunks


def on_device(hidden, cotangent, weight, prev_weight, prev_grad):
    scale = FF ** (-0.5)
    matrix, before, slope = weight[0], prev_weight[0], prev_grad[0]
    rows = matrix.shape[0]
    chunks = row_chunks(rows)

    lefts, rights = [], []
    for at, size in chunks:
        piece = (
            matrix[at : at + size].astype(jnp.float32)
            - 0.5 * before[at : at + size].astype(jnp.float32)
        ).astype(jnp.bfloat16)
        lefts.append(shifted(piece, "replica", 1))
        rights.append(shifted(piece, "replica", -1))

    gathered = gather_rows(hidden[0], "col")
    upstream = gather_rows(cotangent[0], "row")
    partial_value = (
        jnp.dot(gathered, matrix, preferred_element_type=jnp.float32) * scale
    ).astype(jnp.bfloat16)
    output = sum_rows(partial_value, "row")
    term = (
        lax.dot_general(
            upstream, matrix, (((1,), (1,)), ((), ())), preferred_element_type=jnp.float32
        )
        * scale
    )
    hidden_grad = sum_rows(term.astype(jnp.bfloat16), "col")
    grad = (
        lax.dot_general(
            gathered, upstream, (((0,), (0,)), ((), ())), preferred_element_type=jnp.float32
        )
        * scale
    )
    own = (
        matrix.astype(jnp.float32) - 0.5 * before.astype(jnp.float32)
    ).astype(jnp.bfloat16).astype(jnp.float32)
    base = own * (4.0 / 3.0) - 0.5 * (grad - slope.astype(jnp.float32))
    base, output, hidden_grad = lax.optimization_barrier((base, output, hidden_grad))

    fresh = jnp.zeros(matrix.shape, jnp.bfloat16)
    for (at, size), left, right in zip(chunks, lefts, rights):
        around = (left.astype(jnp.float32) + right.astype(jnp.float32)) * (1.0 / 3.0)
        piece = (base[at : at + size] + around).astype(jnp.bfloat16)
        fresh = lax.dynamic_update_slice(fresh, piece, (at, 0))
    return (output[None], hidden_grad[None], fresh[None])


def solution(mesh):
    placed = (
        P("replica", "col", "row"),
        P("replica", "row", "col"),
        P("replica", "row", "col"),
        P("replica", "row", "col"),
        P("replica", "row", "col"),
    )
    return jax.shard_map(
        on_device,
        mesh=mesh,
        in_specs=placed,
        out_specs=(
            P("replica", "row", "col"),
            P("replica", "col", "row"),
            P("replica", "row", "col"),
        ),
        check_vma=False,
    )
```
